128 devices in a mesh: expert: 8 (over x, core), panel: 16 (over y, z).
Axes of the slice: x: 4, y: 4, z: 4, core: 2. Of those that a mesh axis runs over, the one named last changes fastest.
Arguments:
- activations: bfloat16 [2, 128, 96, 6144], P(None, ('expert', 'panel')), may hold values from -6 to 6
- gradients: bfloat16 [2, 128, 96, 16384], P(None, ('expert', 'panel')), may hold values from -6 to 6
- expert_ids: int32 [2, 128, 96, 1], P(None, ('expert', 'panel')), may hold values from 0 to 7; in each aligned block of 96 rows (0 to 95, 96 to 191, ..., all dimensions but the last counted through in order) at most 18 rows name the same one
- sequence_ids: int32 [2, 128, 96], P(None, ('expert', 'panel')), may hold values from 0 to 3, never falling along the last dimension, each value on 1 to 48 neighbouring positions
- input_basis: bfloat16 [8, 6144, 384], P('expert', 'panel'), may hold values from -0.078125 to 0.078125
- output_basis: bfloat16 [8, 16384, 256], P('expert', 'panel'), may hold values from -0.046875 to 0.046875
Outputs:
- corrected_eigenvalues: float32 [8, 384, 256], P('expert', 'panel')
The draws below stay inside these ranges and needn't reach their ends.
Inputs may be any that keep to these rules, and one draw needn't show every extreme that they name: `expert_ids`: among the 96 rows of one device block of one microbatch, no expert is named by more than 18 rows; some block names some expert exactly 18 times; every expert is named somewhere. `sequence_ids`: within a device block of one microbatch the numbers never fall, and each of the 4 sequences holds 1 to 48 rows.
All inputs are finite; a program needn't handle non-finite values.
Results may differ from the reference program's by a relative error of at most 0.00083.
Values may be sent and summed in bfloat16 or wider, within the bound.
A program may use at most 128 MiB of HBM per device.

```python
import math
import jax
import jax.numpy as jnp
import numpy as np
from jax import lax

D = 6144
FF = 16384
EXPERTS = 8
KA = 384
KG = 256
MICRO = 2
SEQ_DEV = 4
TOK_DEV = 96
BLOCKS = 128
CAP = 18
N_EXPERT = 8
N_PANEL = 16


def steps_of(stream_key, dims, shards, smallest, high):
    factor_of, own = 1.0, jax.random.fold_in(stream_key, 6)
    for position, blocks in shards:
        draws = jnp.exp(jax.random.uniform(jax.random.fold_in(own, position), (blocks,), jnp.float32, smallest / len(shards), high / len(shards)))
        factor_of = factor_of * jnp.repeat(draws, dims[position] // blocks).reshape([-1 if axis == position else 1 for axis in range(len(dims))])
    return factor_of


def split_up(count, total, reach, slope):
    loads = [(1 << 20) // math.isqrt(rank ** slope) + 1 for rank in range(2, count + 1)]
    spare, counts = total - reach - (count - 1), [1] * (count - 1)
    while spare > 0:
        free = [i for i in range(count - 1) if counts[i] < reach]
        mass, left = sum([loads[i] for i in free]), spare
        for i in free:
            more = min(reach - counts[i], max(1, left * loads[i] // mass), spare)
            counts[i] = counts[i] + more
            spare = spare - more
    return np.array([reach] + counts)


def ragged(rng, amount, total, reach, skew):
    if amount == 2:
        one = jax.random.randint(rng, (), max(1, total - reach), min(reach, total - 1) + 1)
        return jnp.stack([one, total - one])
    sizes = jnp.asarray(split_up(amount, total, reach, skew), jnp.int32)
    twos = (amount - 1) // 2
    giver, taker = sizes[1:1 + 2 * twos:2], sizes[2:2 + 2 * twos:2]
    margin = jnp.minimum(giver - 1, reach - taker)
    moved = jax.random.randint(jax.random.fold_in(rng, 1), (twos,), 0, 1 << 20) % (margin + 1)
    sizes = sizes.at[1:1 + 2 * twos:2].set(giver - moved).at[2:2 + 2 * twos:2].set(taker + moved)
    return sizes[jax.random.permutation(jax.random.fold_in(rng, 2), amount)]


def routed_block(stream_key, own, number, rows, amount, top, reach, skew):
    ranking = jax.random.permutation(stream_key, amount)
    crowded, common = load_shares(amount, rows * top, reach, skew, True), load_shares(amount, rows * top, reach, skew, False)
    places = jnp.arange(amount)

    def named(tallies, rotation):
        used = int((tallies > 0).sum())
        fixed = max(1, used // 4)
        passed = fixed + (places - fixed + rotation * (used - fixed)) % max(1, amount - fixed)
        return jnp.zeros((amount,), jnp.int32).at[ranking[jnp.where(places < fixed, places, passed)]].set(jnp.asarray(tallies, jnp.int32))

    tallies = jnp.where(number % 4 == 0, named(crowded, number // 4), named(common, number - number // 4 - 1))
    mixed = jax.random.permutation(jax.random.fold_in(own, 3), amount)
    giver, receiver = mixed[0:amount // 2 * 2:2], mixed[1:amount // 2 * 2:2]
    room = jnp.minimum(tallies[giver] - 1, reach - tallies[receiver]) // 2
    room = jnp.where((giver == ranking[0]) | (receiver == ranking[0]) | (tallies[receiver] == 0), 0, jnp.maximum(room, 0))
    passed = jax.random.randint(jax.random.fold_in(own, 4), (amount // 2,), 0, 1 << 20) % (room + 1)
    tallies = tallies.at[giver].add(-passed).at[receiver].add(passed)
    members = jnp.searchsorted(jnp.cumsum(tallies), jnp.arange(rows * top), side="right").astype(jnp.int32)
    table = members.reshape(top, rows).T
    table = table[jax.random.permutation(jax.random.fold_in(own, 1), rows)]
    rotation = jax.random.randint(jax.random.fold_in(own, 2), (rows, 1), 0, top)
    return jnp.take_along_axis(table, (jnp.arange(top)[None, :] + rotation) % top, axis=1)


def load_shares(number_of, total, most, slope, full):
    loads = [(1 << 20) // math.isqrt(standing ** slope) + 1 for standing in range(1, number_of + 1)]
    largest = most if full else min(most, max(-(-total // number_of), total * loads[0] // sum(loads)))
    least = 1 if total - largest >= number_of - 1 else 0
    given, rest = [largest] + [least] * (number_of - 1), total - largest - least * (number_of - 1)
    while rest > 0:
        free = [i for i in range(1, number_of) if given[i] < largest] or [i for i in range(1, number_of) if given[i] < most]
        pool, remaining = sum([loads[i] for i in free]), rest
        for i in free:
            more = min(most - given[i], max(1, remaining * loads[i] // pool), rest)
            given[i] = given[i] + more
            rest = rest - more
    return np.array(given)


def scatter_about(rng, extent, width, limit, cuts=(), held_as=jnp.bfloat16):
    drawn = width * jax.random.normal(rng, extent, jnp.float32)
    if cuts:
        drawn = drawn * steps_of(rng, extent, cuts, -0.22, 0.18)
    return jnp.clip(drawn, -limit, limit).astype(held_as)


def setup_inputs(seed: int = 0) -> dict:
    arg_keys = jax.random.split(jax.random.key(seed), 7)
    activations = scatter_about(arg_keys[0], (MICRO, BLOCKS, TOK_DEV, D), 1.0, 6.0, ((1, 128),))
    gradients = scatter_about(arg_keys[1], (MICRO, BLOCKS, TOK_DEV, FF), 1.0, 6.0, ((1, 128),))
    expert_ids_keys = jax.random.split(jax.random.fold_in(arg_keys[2], 1), MICRO * BLOCKS * TOK_DEV // TOK_DEV)
    expert_ids_turns = jax.random.permutation(jax.random.fold_in(arg_keys[2], 3), MICRO * BLOCKS * TOK_DEV // TOK_DEV)
    expert_ids = jax.vmap(lambda own, number: routed_block(jax.random.fold_in(arg_keys[2], 2), own, number, TOK_DEV, EXPERTS, 1, CAP, 2))(expert_ids_keys, expert_ids_turns).reshape((MICRO, BLOCKS, TOK_DEV, 1))
    sequence_ids = jax.vmap(lambda own: jnp.searchsorted(jnp.cumsum(ragged(own, SEQ_DEV, TOK_DEV, TOK_DEV // 2, 1)), jnp.arange(TOK_DEV), side="right"))(jax.random.split(arg_keys[3], MICRO * BLOCKS)).reshape((MICRO, BLOCKS, TOK_DEV)).astype(jnp.int32)
    input_basis = scatter_about(arg_keys[4], (EXPERTS, D, KA), D ** -0.5, 0.078125, ((0, 8), (1, 16)))
    output_basis = scatter_about(arg_keys[5], (EXPERTS, FF, KG), FF ** -0.5, 0.046875, ((0, 8), (1, 16)))
    return {"activations": activations, "gradients": gradients, "expert_ids": expert_ids, "sequence_ids": sequence_ids, "input_basis": input_basis, "output_basis": output_basis}


def slots_for(inputs, grads, ids, seqs, expert, experts, capacity):
    tokens = ids.shape[0]
    onehot = (ids[:, None] == jnp.arange(experts, dtype=jnp.int32)[None, :]).astype(jnp.int32)
    before = jnp.cumsum(onehot, axis=0) - onehot
    offset = jnp.sum(before * onehot, axis=1).astype(jnp.int32)
    placed = (ids[:, None] == expert) & (offset[:, None] == jnp.arange(capacity, dtype=jnp.int32)[None, :])
    source = jnp.sum(jnp.where(placed, jnp.arange(tokens, dtype=jnp.int32)[:, None], 0), axis=0).astype(jnp.int32)
    filled = jnp.any(placed, axis=0)
    input_rows = jnp.where(filled[:, None], inputs[source], jnp.zeros((), inputs.dtype))
    grad_rows = jnp.where(filled[:, None], grads[source], jnp.zeros((), grads.dtype))
    labels = jnp.where(filled, seqs[source] + 1, 0).astype(jnp.int32)
    return input_rows, grad_rows, labels


def contract(rotated_inputs, rotated_grads, labels, seq_count):
    member = (labels[:, :, None] == jnp.arange(1, seq_count + 1, dtype=jnp.int32)[None, None, :]).astype(jnp.float32)
    masked = jnp.transpose(member, (0, 2, 1))[:, :, :, None] * rotated_inputs.astype(jnp.float32)[:, None, :, :]
    per_seq = jnp.einsum("sjca,scg->sjag", masked, rotated_grads.astype(jnp.float32), precision=lax.Precision.HIGHEST)
    return jnp.sum(per_seq * per_seq, axis=(0, 1))


def reference(activations, gradients, expert_ids, sequence_ids, input_basis, output_basis):
    total = jnp.zeros((EXPERTS, KA, KG), jnp.float32)
    for batch_index in range(MICRO):
        inputs = activations[batch_index]
        grads = gradients[batch_index]
        ids = expert_ids[batch_index, :, :, 0]
        seqs = sequence_ids[batch_index]

        def per_expert(packed):
            expert, basis_a, basis_g = packed
            input_rows, grad_rows, labels = jax.vmap(
                lambda one_in, one_grad, one_ids, one_seqs: slots_for(one_in, one_grad, one_ids, one_seqs, expert, EXPERTS, CAP)
            )(inputs, grads, ids, seqs)
            flat_in = input_rows.reshape(BLOCKS * CAP, D)
            flat_grad = grad_rows.reshape(BLOCKS * CAP, FF)
            rotated_in = jnp.dot(flat_in, basis_a, preferred_element_type=jnp.float32).astype(jnp.bfloat16)
            rotated_out = jnp.dot(flat_grad, basis_g, preferred_element_type=jnp.float32).astype(jnp.bfloat16)
            rotated_in = rotated_in.reshape(N_EXPERT, N_PANEL, CAP, KA)
            rotated_out = rotated_out.reshape(N_EXPERT, N_PANEL, CAP, KG)
            grouped = labels.reshape(N_EXPERT, N_PANEL, CAP)
            partial_sums = lax.map(lambda group: contract(group[0], group[1], group[2], SEQ_DEV), (rotated_in, rotated_out, grouped))
            return jnp.sum(partial_sums, axis=0)

        total = total + lax.map(per_expert, (jnp.arange(EXPERTS, dtype=jnp.int32), input_basis, output_basis))
    return total / (MICRO * BLOCKS * SEQ_DEV)
```

```python
import functools

import jax
import jax.numpy as jnp
from jax import lax
from jax.experimental import pallas as pl
from jax.experimental.pallas import tpu as pltpu
from jax.sharding import PartitionSpec as P

MESH = pl.DeviceIdType.MESH
SEQS = 4
N = 4
CAP = 18
PAIR = 48
TAG = 1024
BF16 = jnp.bfloat16
F32 = jnp.float32


def kernel(sizes, *refs):
    (codes, act, grad, ibs, gbs, out) = refs[:6]
    (cz, cy, gx, ix, gb, ib, pg, pi, go, io, rg, ri, rs, ra, acc, fr) = refs[6:22]
    (s_send, s_cz, s_cy, s_gx, s_ix, s_loc, s_a, s_p, s_rg, s_ri, s_ra, s_fr) = refs[22:]
    toks, wa, wg, ka, kg, rows = sizes
    ga, gg = wa // N, wg // N
    pa, pgc = ga // N, gg // N
    e = lax.axis_index("expert")
    p = lax.axis_index("panel")
    x, c = e // 2, e % 2
    y, z = p // N, p % N
    other = 1 - c

    def dev(xx, yy, zz, cc):
        return (2 * xx + cc, N * yy + zz)

    def up(i, d):
        return (i + d) % N

    sends = []

    def send(src, dst, sem, device, when=None):
        i = len(sends)
        copy = pltpu.make_async_remote_copy(
            src_ref=src,
            dst_ref=dst,
            send_sem=s_send.at[i],
            recv_sem=sem,
            device_id=device,
            device_id_type=MESH,
        )
        sends.append((copy, when))
        if when is None:
            copy.start()
        else:
            pl.when(when)(lambda: copy.start())

    def arrived(ref, sem):
        pltpu.make_async_copy(ref, ref, sem).wait()

    barrier = pltpu.get_barrier_semaphore()
    total = N * N * N

    def greet(i, _):
        xx, yy, zz = up(x, i // (N * N)), up(y, (i // N) % N), up(z, i % N)
        pl.semaphore_signal(
            barrier, inc=1, device_id=dev(xx, yy, zz, c), device_id_type=MESH
        )
        return _

    lax.fori_loop(1, total, greet, 0)
    for d in range(N):
        pl.semaphore_signal(
            barrier, inc=1, device_id=dev(x, up(y, d), z, other), device_id_type=MESH
        )
    for d in range(1, N):
        pl.semaphore_signal(
            barrier, inc=1, device_id=dev(x, y, up(z, d), other), device_id_type=MESH
        )
    pl.semaphore_wait(barrier, total - 1 + N + N - 1)

    slot_z, slot_y = 2 * z + c, 2 * y + c
    for d in range(N):
        for cc in (c, other):
            if d == 0 and cc is c:
                continue
            send(codes, cz.at[slot_z], s_cz.at[slot_z], dev(x, y, up(z, d), cc))
            send(codes, cy.at[slot_y], s_cy.at[slot_y], dev(x, up(y, d), z, cc))

    half = pgc // 2

    class Gather:
        def __init__(self, k, hbm, at, row, n, i1, i2, dev1, dev2):
            self.k, self.at, self.row, self.n = k, at, row, n
            self.i1, self.i2, self.dev1, self.dev2 = i1, i2, dev1, dev2
            self.own = hbm.at[0, pl.ds(row, n)]

        def first(self):
            for d in (1, 3, 2):
                send(
                    self.own,
                    self.at(self.i1, self.i2, self.row, self.n),
                    s_a.at[self.k, self.i1],
                    self.dev1(up(self.i1, d)),
                )

        def second(self, d):
            j = up(self.i1, d)
            src = self.own
            land = self.at(j, self.i2, self.row, self.n)
            if d:
                arrived(land, s_a.at[self.k, j])
                src = land
            send(src, land, s_p.at[self.k, j, 0], self.dev2(up(self.i2, 1)))
            send(src, land, s_p.at[self.k, j, 1], self.dev2(up(self.i2, 3)))

        def relay(self, d):
            j = up(self.i1, d)
            h = self.n // 2
            left, right = up(self.i2, 3), up(self.i2, 1)
            arrived(self.at(j, left, self.row, self.n), s_p.at[self.k, j, 0])
            piece = self.at(j, left, self.row, h)
            send(piece, piece, s_p.at[self.k, j, 2], self.dev2(right))
            arrived(self.at(j, right, self.row, self.n), s_p.at[self.k, j, 1])
            piece = self.at(j, right, self.row + h, h)
            send(piece, piece, s_p.at[self.k, j, 3], self.dev2(left))

        def last(self, d):
            j = up(self.i1, d)
            h = self.n // 2
            far = up(self.i2, 2)
            arrived(self.at(j, far, self.row, h), s_p.at[self.k, j, 2])
            arrived(self.at(j, far, self.row + h, h), s_p.at[self.k, j, 3])

    along_x = lambda j: dev(j, y, z, c)
    along_y = lambda j: dev(x, j, z, c)
    along_z = lambda j: dev(x, y, j, c)
    gb0 = Gather(
        0, gbs, lambda j1, j2, r, n: gb.at[j1, j2, pl.ds(r, n)], 0, half, x, y, along_x, along_y
    )
    gb1 = Gather(
        1, gbs, lambda j1, j2, r, n: gb.at[j2, j1, pl.ds(r, n)], half, half, y, x, along_y, along_x
    )
    ibz = Gather(
        2, ibs, lambda j1, j2, r, n: ib.at[j2, j1, pl.ds(r, n)], 0, pa, z, x, along_z, along_x
    )

    gb0.first()
    gb1.first()
    ibz.first()

    def grad_part(b, zz, k):
        return grad.at[b, 0, :, pl.ds(pl.multiple_of((k * N + zz) * pgc, pgc), pgc)]

    def act_part(b, yy):
        return act.at[b, 0, :, pl.ds(pl.multiple_of(yy * ga, ga), ga)]

    def gx_part(b, k):
        return gx.at[slot_z, b, :, pl.ds(k * pgc, pgc)]

    def send_grad(b, d):
        for k in range(N):
            send(
                grad_part(b, up(z, d), k), gx_part(b, k), s_gx.at[b, slot_z], along_z(up(z, d))
            )

    def send_act(b, d):
        send(act_part(b, up(y, d)), ix.at[slot_y, b], s_ix.at[b, slot_y], along_y(up(y, d)))

    def own_rows(b):
        for k in range(N):
            pltpu.make_async_copy(grad_part(b, z, k), gx_part(b, k), s_loc.at[b]).start()
            send(grad_part(b, z, k), gx_part(b, k), s_gx.at[b, slot_z], dev(x, y, z, other))
        pltpu.make_async_copy(act_part(b, y), ix.at[slot_y, b], s_loc.at[2 + b]).start()
        send(act_part(b, y), ix.at[slot_y, b], s_ix.at[b, slot_y], dev(x, y, z, other))

    for d in (1, 3, 2):
        send_act(0, d)
    for d in (1, 3, 2):
        send_grad(0, d)
    own_rows(0)
    pltpu.make_async_copy(gbs.at[0], gb.at[x, y], s_loc.at[4]).start()
    pltpu.make_async_copy(ibs.at[0], ib.at[x, z], s_loc.at[5]).start()
    cz[slot_z] = codes[...]
    cy[slot_y] = codes[...]
    for d in (1, 3, 2):
        send_grad(1, d)
    own_rows(1)

    for d in range(N):
        gb0.second(d)
        gb1.second(d)
        ibz.second(d)
    for d in (1, 3, 2):
        send_act(1, d)

    for d in range(N):
        for cc in (c, other):
            if d == 0 and cc is c:
                continue
            sz, sy = 2 * up(z, d) + cc, 2 * up(y, d) + cc
            arrived(cz.at[sz], s_cz.at[sz])
            arrived(cy.at[sy], s_cy.at[sy])

    def hand_on(buf, sem, b, q):
        s = 2 * q + c
        arrived(buf.at[s, b], sem.at[b, s])
        send(buf.at[s, b], buf.at[s, b], sem.at[b, s], dev(x, y, z, other))

    slots = N * PAIR

    def pack(buf, sem, code, dst, b, q, chunk):
        s = 2 * q + other
        arrived(buf.at[s, b], sem.at[b, s])
        numbers = code[2 * q, b : b + 1, : 2 * toks] + code[2 * q + 1, b : b + 1, : 2 * toks]
        mine = lax.broadcasted_iota(jnp.int32, (slots, 2 * toks), 0) + (1 + c * TAG)
        place = jnp.where(numbers == mine, 1.0, 0.0).astype(BF16)

        def step(i, _):
            cols = pl.ds(pl.multiple_of(i * chunk, chunk), chunk)
            block = buf[pl.ds(2 * q, 2), b, :, cols].reshape(2 * toks, chunk)
            packed = jnp.dot(place, block, preferred_element_type=F32).astype(BF16)
            dst[b, :, q, :, cols] = packed.reshape(N, PAIR, chunk)
            return _

        lax.fori_loop(0, buf.shape[3] // chunk, step, 0)

    def pack_grad(b, q):
        pack(gx, s_gx, cz, pg, b, q, 512)

    def pack_act(b, q):
        pack(ix, s_ix, cy, pi, b, q, 512)

    def local_rows(b):
        for k in range(N):
            arrived(gx_part(b, k), s_loc.at[b])
        arrived(ix.at[slot_y, b], s_loc.at[2 + b])

    local_rows(0)
    for d in (1, 3, 2):
        hand_on(ix, s_ix, 0, up(y, d))
    for d in (1, 3):
        hand_on(gx, s_gx, 0, up(z, d))
    for d in (0, 1, 3, 2):
        pack_act(0, up(y, d))
    for d in (0, 1, 3):
        pack_grad(0, up(z, d))
    for d in (0, 1):
        gb0.relay(d)
        gb1.relay(d)
        ibz.relay(d)
    hand_on(gx, s_gx, 0, up(z, 2))
    for d in (2, 3):
        gb0.relay(d)
        gb1.relay(d)
        ibz.relay(d)
    pack_grad(0, up(z, 2))
    local_rows(1)
    for d in (1, 3):
        hand_on(gx, s_gx, 1, up(z, d))
    for d in (0, 1, 3):
        pack_grad(1, up(z, d))
    for d in (1, 3, 2):
        hand_on(ix, s_ix, 1, up(y, d))
    for d in (0, 1, 3, 2):
        pack_act(1, up(y, d))
    arrived(gb.at[x, y], s_loc.at[4])
    arrived(ib.at[x, z], s_loc.at[5])
    for d in range(N):
        gb0.last(d)
        gb1.last(d)
        ibz.last(d)

    def rotate(b):
        def one(k, _):
            t = jnp.zeros((slots, ka), F32)
            for j in range(N):
                block = pi[b, k, :, :, j * pa : (j + 1) * pa].reshape(slots, pa)
                t += jnp.dot(block, ib[k, j], preferred_element_type=F32)
            io[b, k] = t.astype(BF16)
            return _

        lax.fori_loop(0, N, one, 0)

        for d in (1, 3, 2):
            k = up(y, d)
            send(io.at[b, k], ri.at[b, y], s_ri.at[b, y], along_y(k))

        def two(k, _):
            t = jnp.zeros((slots, kg), F32)
            for j in range(N):
                block = pg[b, k, :, :, j * pgc : (j + 1) * pgc].reshape(slots, pgc)
                t += jnp.dot(block, gb[k, j], preferred_element_type=F32)
            go[b, k] = t.astype(BF16)
            return _

        lax.fori_loop(0, N, two, 0)

        for d in (1, 3, 2):
            k = up(z, d)
            send(go.at[b, k], rg.at[b, z], s_rg.at[b, z], along_z(k))

    stays = y == z

    def owners(b):
        t = io[b, y].astype(F32)
        for d in (1, 3, 2):
            k = up(y, d)
            arrived(ri.at[b, k], s_ri.at[b, k])
            t += ri[b, k].astype(F32)
        rs[b] = t.astype(BF16).reshape(N, PAIR, ka)
        for d in (1, 3, 2, 0):
            k = up(y, d)
            send(
                rs.at[b, k],
                ra.at[b, z],
                s_ra.at[b, z],
                dev(x, k, y, c),
                when=None if d else jnp.logical_not(stays),
            )

        @pl.when(stays)
        def _():
            ra[b, z] = rs[b, y]

    def contract(b):
        t = go[b, z].astype(F32)
        for d in (1, 3, 2):
            k = up(z, d)
            arrived(rg.at[b, k], s_rg.at[b, k])
            t += rg[b, k].astype(F32)
        rg[b, z] = t.astype(BF16)

        for d in range(N):
            k = up(z, d)
            if d == 0:
                pl.when(jnp.logical_not(stays))(lambda: arrived(ra.at[b, k], s_ra.at[b, k]))
            else:
                arrived(ra.at[b, k], s_ra.at[b, k])

        def one(k, _):
            numbers = cz[2 * k, b : b + 1, : 2 * toks] + cz[2 * k + 1, b : b + 1, : 2 * toks]
            labels = (
                cz[2 * k, 2 + b : 3 + b, : 2 * toks] + cz[2 * k + 1, 2 + b : 3 + b, : 2 * toks]
            )
            mine = lax.broadcasted_iota(jnp.int32, (PAIR, 2 * toks), 0) + (
                1 + c * TAG + z * PAIR
            )
            label = jnp.sum(jnp.where(numbers == mine, labels, 0), axis=1, keepdims=True)
            left = ra[b, k].astype(F32).T.astype(BF16)
            right = rg[b, z, pl.ds(pl.multiple_of(k * PAIR, PAIR), PAIR), :].astype(F32)
            for r in range(0, ka, 96):
                rows_of = left[r : r + 96]
                t = jnp.zeros((96, kg), F32)
                for g in range(1, 2 * SEQS + 1):
                    masked = jnp.where(label == g, right, 0.0).astype(BF16)
                    o = jnp.dot(rows_of, masked, preferred_element_type=F32)
                    t += o * o
                acc[r // rows : (r + 96) // rows] += t.reshape(96 // rows, rows, kg)
            return _

        lax.fori_loop(0, N, one, 0)

    acc[...] = jnp.zeros_like(acc)
    rotate(0)
    hand_on(gx, s_gx, 1, up(z, 2))
    owners(0)
    pack_grad(1, up(z, 2))
    rotate(1)
    contract(0)
    owners(1)
    contract(1)

    here = x == z
    mine = N * x + y
    for dy in range(N):
        for dz in range(N):
            yy, zz = up(y, dy), up(z, dz)
            send(
                acc.at[N * yy + zz],
                fr.at[mine],
                s_fr.at[mine],
                dev(z, yy, zz, c),
                when=None if dy or dz else jnp.logical_not(here),
            )

    @pl.when(here)
    def _():
        fr[mine] = acc[p]

    t = jnp.zeros((rows, kg), F32)
    for dx in range(N):
        for dy in range(N):
            k = N * up(x, dx) + up(y, dy)
            if dx or dy:
                arrived(fr.at[k], s_fr.at[k])
            else:
                pl.when(jnp.logical_not(here))(lambda: arrived(fr.at[k], s_fr.at[k]))
    for k in range(N * N):
        t += fr[k]
    out[...] = t * (1.0 / (2 * 128 * SEQS))

    for copy, when in sends:
        if when is None:
            copy.wait_send()
        else:
            pl.when(when)(lambda copy=copy: copy.wait_send())


def slot_numbers(ids, seqs):
    toks = ids.shape[1]
    c = lax.axis_index("expert") % 2
    order = jnp.arange(toks, dtype=jnp.int32)
    earlier = (ids[:, :, None] == ids[:, None, :]) & (order[None, :] < order[:, None])[None]
    offset = jnp.sum(earlier.astype(jnp.int32), axis=2)
    number = (ids % 2) * TAG + (ids // 2) * PAIR + offset + 1 + c * CAP
    label = seqs + 1 + SEQS * c
    both = jnp.concatenate([number, label], axis=0)
    width = 256
    first = jnp.pad(both, ((0, 4), (0, width - toks)))
    second = jnp.pad(both, ((0, 4), (toks, width - 2 * toks)))
    return jnp.where(c == 0, first, second)


def per_device(activations, gradients, expert_ids, sequence_ids, input_basis, output_basis):
    micro, _, toks, wa = activations.shape
    wg = gradients.shape[3]
    pa, ka = input_basis.shape[1:]
    pgc, kg = output_basis.shape[1:]
    rows = ka // (N * N)
    codes = slot_numbers(expert_ids[:, 0, :, 0], sequence_ids[:, 0])
    slots = N * PAIR
    vmem = pltpu.VMEM
    dma = pltpu.SemaphoreType.DMA
    anywhere = pl.BlockSpec(memory_space=pl.ANY)
    return pl.pallas_call(
        functools.partial(kernel, (toks, wa, wg, ka, kg, rows)),
        out_shape=jax.ShapeDtypeStruct((rows, kg), F32),
        in_specs=[pl.BlockSpec(memory_space=vmem)] + [anywhere] * 4,
        out_specs=pl.BlockSpec(memory_space=vmem),
        scratch_shapes=[
            vmem((2 * N, 8, 256), jnp.int32),
            vmem((2 * N, 8, 256), jnp.int32),
            vmem((2 * N, micro, toks, wg // N), BF16),
            vmem((2 * N, micro, toks, wa // N), BF16),
            vmem((N, N, pgc, kg), BF16),
            vmem((N, N, pa, ka), BF16),
            vmem((micro, N, N, PAIR, wg // N), BF16),
            vmem((micro, N, N, PAIR, wa // N), BF16),
            vmem((micro, N, slots, kg), BF16),
            vmem((micro, N, slots, ka), BF16),
            vmem((micro, N, slots, kg), BF16),
            vmem((micro, N, slots, ka), BF16),
            vmem((micro, N, PAIR, ka), BF16),
            vmem((micro, N, PAIR, ka), BF16),
            vmem((N * N, rows, kg), F32),
            vmem((N * N, rows, kg), F32),
            dma((192,)),
            dma((2 * N,)),
            dma((2 * N,)),
            dma((micro, 2 * N)),
            dma((micro, 2 * N)),
            dma((6,)),
            dma((3, N)),
            dma((3, N, 4)),
            dma((micro, N)),
            dma((micro, N)),
            dma((micro, N)),
            dma((N * N,)),
        ],
        compiler_params=pltpu.CompilerParams(
            collective_id=0, has_side_effects=True, vmem_limit_bytes=63 << 20
        ),
        name="eigen",
    )(codes, activations, gradients, input_basis, output_basis)[None]


def solution(mesh):
    placed = (
        P(None, ("expert", "panel"), None, None),
        P(None, ("expert", "panel"), None, None),
        P(None, ("expert", "panel"), None, None),
        P(None, ("expert", "panel"), None),
        P("expert", "panel", None),
        P("expert", "panel", None),
    )
    return jax.shard_map(
        per_device,
        mesh=mesh,
        in_specs=placed,
        out_specs=P("expert", "panel", None),
        check_vma=False,
    )
```

```python
import functools

import jax
import jax.numpy as jnp
from jax import lax
from jax.experimental import pallas as pl
from jax.experimental.pallas import tpu as pltpu
from jax.sharding import PartitionSpec as P

MESH = pl.DeviceIdType.MESH
SEQS = 4
N = 4
CAP = 18
PAIR = 48
NEAR = (0, 1, 3, 2)
TAG = 1024
BF16 = jnp.bfloat16
F32 = jnp.float32


def kernel(sizes, *refs):
    (ids, seqs, act, grad, ibs, gbs, out) = refs[:7]
    (lanes, codes, cz, cy, gx, ix, gb, ib, pg, pi, go, io, rg, ri, rs, ra, acc, fr) = refs[7:25]
    (s_send, s_cz, s_cy, s_gx, s_ix, s_loc, s_a, s_f, s_p, s_rg, s_ri, s_ra, s_fr) = refs[25:]
    toks, wa, wg, ka, kg, rows = sizes
    ga, gg = wa // N, wg // N
    pa, pgc = ga // N, gg // N
    e = lax.axis_index("expert")
    p = lax.axis_index("panel")
    x, c = e // 2, e % 2
    y, z = p // N, p % N
    other = 1 - c

    def dev(xx, yy, zz, cc):
        return (2 * xx + cc, N * yy + zz)

    def up(i, d):
        return (i + d) % N

    sends = []

    def send(src, dst, sem, device, when=None):
        i = len(sends)
        copy = pltpu.make_async_remote_copy(
            src_ref=src,
            dst_ref=dst,
            send_sem=s_send.at[i],
            recv_sem=sem,
            device_id=device,
            device_id_type=MESH,
        )
        sends.append((copy, when))
        if when is None:
            copy.start()
        else:
            pl.when(when)(lambda: copy.start())

    def sent(some):
        for copy, when in some:
            if when is None:
                copy.wait_send()
            else:
                pl.when(when)(lambda copy=copy: copy.wait_send())

    def arrived(ref, sem):
        pltpu.make_async_copy(ref, ref, sem).wait()

    held = up(z, N - x)
    here = x == held
    barrier = pltpu.get_barrier_semaphore()

    def greet(*device):
        pl.semaphore_signal(barrier, inc=1, device_id=dev(*device), device_id_type=MESH)

    xs, ys, zs = ([up(i, d) for d in range(N)] for i in (x, y, z))
    for d in range(1, N):
        greet(x, ys[d], z, other)
        greet(x, y, zs[d], other)
    greet(x, y, z, other)
    for dx in (2, 1, 3, 0):
        for dy in (2, 1, 3, 0):
            for dz in (2, 1, 3, 0):
                if dx or dy or dz:
                    greet(xs[dx], ys[dy], zs[dz], c)

    codes[...] = jnp.zeros_like(codes)
    lanes[...] = jnp.full_like(lanes, -1.0)
    above = lax.broadcasted_iota(jnp.int32, (2 * toks, 2 * toks), 0) < lax.broadcasted_iota(
        jnp.int32, (2 * toks, 2 * toks), 1
    )
    for b in range(2):
        for cc in range(2):

            @pl.when(c == cc)
            def _():
                lanes[b : b + 1, cc * toks : (cc + 1) * toks] = ids[b].astype(F32)

        row = lanes[b : b + 1, : 2 * toks]
        column = jnp.broadcast_to(row, (8, 2 * toks)).T[:, :1]
        earlier = jnp.logical_and(column == row, above)
        offset = jnp.sum(jnp.where(earlier, 1.0, 0.0), axis=0, keepdims=True).astype(jnp.int32)
        expert = row.astype(jnp.int32)
        number = (expert & 1) * TAG + (expert >> 1) * PAIR + offset + (1 + c * CAP)
        codes[b : b + 1, : 2 * toks] = jnp.where(expert < 0, 0, number)
    for cc in range(2):

        @pl.when(c == cc)
        def _():
            codes[2:4, cc * toks : (cc + 1) * toks] = seqs[:, 0] + (1 + SEQS * cc)

    pl.semaphore_wait(barrier, N * N * N + 2 * (N - 1))

    slot_z, slot_y = 2 * z + c, 2 * y + c
    for d in range(N):
        for cc in (c, other):
            if d == 0 and cc is c:
                continue
            send(codes, cz.at[slot_z], s_cz.at[slot_z], dev(x, y, up(z, d), cc))
            send(codes, cy.at[slot_y], s_cy.at[slot_y], dev(x, up(y, d), z, cc))

    cut = pgc * 5 // 8

    class Gather:
        def __init__(self, k, hbm, at, row, n, i1, i2, dev1, dev2, direct):
            self.direct = direct
            self.k, self.at, self.row, self.n = k, at, row, n
            self.i1, self.i2, self.dev1, self.dev2 = i1, i2, dev1, dev2
            self.own = hbm.at[0, pl.ds(row, n)]

        def first(self):
            for d in (1, 3, 2) if self.direct else (1, 3):
                send(
                    self.own,
                    self.at(self.i1, self.i2, self.row, self.n),
                    s_a.at[self.k, self.i1],
                    self.dev1(up(self.i1, d)),
                )

        def first_relay(self):
            h = self.n // 2
            for d, row in ((3, self.row), (1, self.row + h)):
                j = up(self.i1, d)
                arrived(self.at(j, self.i2, self.row, self.n), s_a.at[self.k, j])
                piece = self.at(j, self.i2, row, h)
                send(piece, piece, s_f.at[self.k, d // 2], self.dev1(up(self.i1, N - d)))

        def second(self, d):
            j = up(self.i1, d)
            land = self.at(j, self.i2, self.row, self.n)
            src = land if d else self.own
            if d and (self.direct or d != 2):
                if self.direct:
                    arrived(land, s_a.at[self.k, j])
            elif d:
                h = self.n // 2
                arrived(self.at(j, self.i2, self.row, h), s_f.at[self.k, 1])
                arrived(self.at(j, self.i2, self.row + h, h), s_f.at[self.k, 0])
            send(src, land, s_p.at[self.k, j, 0], self.dev2(up(self.i2, 1)))
            send(src, land, s_p.at[self.k, j, 1], self.dev2(up(self.i2, 3)))

        def relay(self, d):
            j = up(self.i1, d)
            h = self.n // 2
            left, right = up(self.i2, 3), up(self.i2, 1)
            arrived(self.at(j, left, self.row, self.n), s_p.at[self.k, j, 0])
            piece = self.at(j, left, self.row, h)
            send(piece, piece, s_p.at[self.k, j, 2], self.dev2(right))
            arrived(self.at(j, right, self.row, self.n), s_p.at[self.k, j, 1])
            piece = self.at(j, right, self.row + h, h)
            send(piece, piece, s_p.at[self.k, j, 3], self.dev2(left))

        def last(self, d):
            j = up(self.i1, d)
            h = self.n // 2
            far = up(self.i2, 2)
            arrived(self.at(j, far, self.row, h), s_p.at[self.k, j, 2])
            arrived(self.at(j, far, self.row + h, h), s_p.at[self.k, j, 3])

    along_x = lambda j: dev(j, y, z, c)
    along_y = lambda j: dev(x, j, z, c)
    along_z = lambda j: dev(x, y, j, c)
    gb0 = Gather(
        0, gbs, lambda j1, j2, r, n: gb.at[j1, j2, pl.ds(r, n)], 0, cut, x, y, along_x, along_y, False
    )
    gb1 = Gather(
        1, gbs, lambda j1, j2, r, n: gb.at[j2, j1, pl.ds(r, n)], cut, pgc - cut, y, x, along_y, along_x, False
    )
    ibz = Gather(
        2, ibs, lambda j1, j2, r, n: ib.at[j2, j1, pl.ds(r, n)], 0, pa, z, x, along_z, along_x, True
    )

    gb0.first()
    gb1.first()
    ibz.first()

    def grad_part(b, zz, k):
        return grad.at[b, 0, :, pl.ds(pl.multiple_of((k * N + zz) * pgc, pgc), pgc)]

    def act_part(b, yy):
        return act.at[b, 0, :, pl.ds(pl.multiple_of(yy * ga, ga), ga)]

    def gx_part(b, k):
        return gx.at[slot_z, b, :, pl.ds(k * pgc, pgc)]

    def send_grad(b, d):
        for k in range(N):
            send(
                grad_part(b, up(z, d), k), gx_part(b, k), s_gx.at[b, slot_z], along_z(up(z, d))
            )

    def send_act(b, d):
        send(act_part(b, up(y, d)), ix.at[slot_y, b], s_ix.at[b, slot_y], along_y(up(y, d)))

    def own_rows(b):
        for k in range(N):
            pltpu.make_async_copy(grad_part(b, z, k), gx_part(b, k), s_loc.at[b]).start()
            send(grad_part(b, z, k), gx_part(b, k), s_gx.at[b, slot_z], dev(x, y, z, other))
        pltpu.make_async_copy(act_part(b, y), ix.at[slot_y, b], s_loc.at[2 + b]).start()
        send(act_part(b, y), ix.at[slot_y, b], s_ix.at[b, slot_y], dev(x, y, z, other))

    for d in (1, 3, 2):
        send_grad(0, d)
    ibz.second(0)
    gb0.second(0)
    gb0.first_relay()
    gb1.first_relay()
    for d in (1, 3, 2):
        send_act(0, d)
    gb1.second(0)
    own_rows(0)
    pltpu.make_async_copy(gbs.at[0], gb.at[x, y], s_loc.at[4]).start()
    pltpu.make_async_copy(ibs.at[0], ib.at[x, z], s_loc.at[5]).start()
    cz[slot_z] = codes[...]
    cy[slot_y] = codes[...]
    for d in (1, 3, 2):
        send_grad(1, d)
    own_rows(1)

    for d in (1, 3, 2):
        ibz.second(d)
        gb0.second(d)
    for d in (1, 3, 2):
        gb1.second(d)
    for d in (1, 3, 2):
        send_act(1, d)

    for d in range(N):
        for cc in (c, other):
            if d == 0 and cc is c:
                continue
            sz, sy = 2 * up(z, d) + cc, 2 * up(y, d) + cc
            arrived(cz.at[sz], s_cz.at[sz])
            arrived(cy.at[sy], s_cy.at[sy])

    def hand_on(buf, sem, b, q):
        s = 2 * q + c
        arrived(buf.at[s, b], sem.at[b, s])
        send(buf.at[s, b], buf.at[s, b], sem.at[b, s], dev(x, y, z, other))

    slots = N * PAIR

    def pack(buf, sem, code, dst, b, q, pos, chunk):
        s = 2 * q + other
        arrived(buf.at[s, b], sem.at[b, s])
        numbers = code[2 * q, b : b + 1, : 2 * toks] + code[2 * q + 1, b : b + 1, : 2 * toks]
        mine = lax.broadcasted_iota(jnp.int32, (slots, 2 * toks), 0) + (1 + c * TAG)
        place = jnp.where(numbers == mine, 1.0, 0.0).astype(BF16)

        def step(i, _):
            cols = pl.ds(pl.multiple_of(i * chunk, chunk), chunk)
            block = buf[pl.ds(2 * q, 2), b, :, cols].reshape(2 * toks, chunk)
            packed = jnp.dot(place, block, preferred_element_type=F32).astype(BF16)
            dst[b, :, pos, :, cols] = packed.reshape(N, PAIR, chunk)
            return _

        lax.fori_loop(0, buf.shape[3] // chunk, step, 0)

    def pack_grad(b, d):
        pack(gx, s_gx, cz, pg, b, up(z, d), NEAR.index(d), 512)

    def pack_act(b, d):
        pack(ix, s_ix, cy, pi, b, up(y, d), NEAR.index(d), 512)

    def local_rows(b):
        for k in range(N):
            arrived(gx_part(b, k), s_loc.at[b])
        arrived(ix.at[slot_y, b], s_loc.at[2 + b])

    def rotate(src, basis, dst, b, k, lo, hi):
        depth = basis.shape[2]
        m = (hi - lo) * PAIR
        t = jnp.zeros((m, basis.shape[3]), F32)
        for j in range(N):
            block = src[b, k, lo:hi, :, j * depth : (j + 1) * depth].reshape(m, depth)
            t += jnp.dot(block, basis[k, j], preferred_element_type=F32)
        dst[b, k, lo:hi] = t.astype(BF16).reshape(hi - lo, PAIR, basis.shape[3])

    def rotate_in(b, experts):
        for d in experts:
            rotate(pi, ib, io, b, up(x, d), 0, N)

    def rotate_out(b, experts, lo, hi):
        for d in experts:
            rotate(pg, gb, go, b, up(x, d), lo, hi)

    def share(src, dst, sem, me, along, b, experts, lo, hi):
        for d in experts:
            k = up(x, d)
            owner = (k + x) % N
            for i in range(lo, hi):
                send(
                    src.at[b, k, i],
                    dst.at[b, me, up(me, NEAR[i])],
                    sem.at[b, me],
                    along(owner),
                    when=owner != me,
                )

    def share_in(b, experts):
        share(io, ri, s_ri, y, along_y, b, experts, 0, N)

    def share_out(b, experts, lo, hi):
        share(go, rg, s_rg, z, along_z, b, experts, lo, hi)

    close, far = NEAR[:3], NEAR[3:]

    local_rows(0)
    for d in (1, 3, 2):
        hand_on(ix, s_ix, 0, up(y, d))
    for d in (1, 3):
        hand_on(gx, s_gx, 0, up(z, d))
    for d in NEAR:
        pack_act(0, d)
    arrived(ib.at[x, z], s_loc.at[5])
    for d in close:
        pack_grad(0, d)
    for d in NEAR:
        ibz.relay(d)
    rotate_in(0, close)
    share_in(0, close)
    hand_on(gx, s_gx, 0, up(z, 2))
    for d in NEAR:
        gb0.relay(d)
    pack_grad(0, 2)
    local_rows(1)
    for d in (1, 3, 2):
        hand_on(ix, s_ix, 1, up(y, d))
    for d in NEAR:
        gb1.relay(d)
    for d in NEAR:
        pack_act(1, d)
    rotate_in(1, close)
    share_in(1, close)
    for d in (1, 3):
        hand_on(gx, s_gx, 1, up(z, d))
    for d in close:
        pack_grad(1, d)
    for d in NEAR:
        ibz.last(d)
    for b in range(2):
        rotate_in(b, far)
        share_in(b, far)
    arrived(gb.at[x, y], s_loc.at[4])
    for d in close:
        gb0.last(d)
        rotate_out(0, (d,), 0, N)
        rotate_out(1, (d,), 0, 3)
        share_out(0, (d,), 0, N)
        share_out(1, (d,), 0, 3)
    gb0.last(2)
    for d in range(N):
        gb1.last(d)
    rotate_out(0, far, 0, N)
    rotate_out(1, far, 0, 3)
    share_out(0, far, 0, N)
    share_out(1, far, 0, 3)
    hand_on(gx, s_gx, 1, up(z, 2))
    pack_grad(1, 2)
    rotate_out(1, NEAR, 3, N)
    share_out(1, NEAR, 3, N)

    def owned(src, dst, sem, me, b, store):
        for d in (1, 3, 2):
            k = up(me, d)
            arrived(dst.at[b, k], sem.at[b, k])
        for i, d in enumerate(NEAR):
            q = up(me, d)
            t = src[b, up(me, N - x), i].astype(F32)
            for j in (1, 3, 2):
                t += dst[b, up(me, j), q].astype(F32)
            store(q, t.astype(BF16))

    stays = y == z

    def owners(b):
        def store(q, value):
            rs[b, q] = value

        owned(io, ri, s_ri, y, b, store)
        for d in (1, 3, 2, 0):
            k = up(y, d)
            send(
                rs.at[b, k],
                ra.at[b, z],
                s_ra.at[b, z],
                dev(x, k, y, c),
                when=None if d else jnp.logical_not(stays),
            )

        @pl.when(stays)
        def _():
            ra[b, z] = rs[b, y]

    def contract(b):
        def store(q, value):
            rg[b, z, q] = value

        owned(go, rg, s_rg, z, b, store)
        for d in range(N):
            k = up(z, d)
            if d == 0:
                pl.when(jnp.logical_not(stays))(lambda: arrived(ra.at[b, k], s_ra.at[b, k]))
            else:
                arrived(ra.at[b, k], s_ra.at[b, k])

        def one(k, _):
            numbers = cz[2 * k, b : b + 1, : 2 * toks] + cz[2 * k + 1, b : b + 1, : 2 * toks]
            labels = (
                cz[2 * k, 2 + b : 3 + b, : 2 * toks] + cz[2 * k + 1, 2 + b : 3 + b, : 2 * toks]
            )
            mine = lax.broadcasted_iota(jnp.int32, (PAIR, 2 * toks), 0) + (
                1 + c * TAG + up(z, N - x) * PAIR
            )
            label = jnp.sum(jnp.where(numbers == mine, labels, 0), axis=1, keepdims=True)
            left = ra[b, k].astype(F32).T.astype(BF16)
            right = rg[b, z, k].astype(F32)
            for r in range(0, ka, 96):
                rows_of = left[r : r + 96]
                t = jnp.zeros((96, kg), F32)
                for g in range(1, 2 * SEQS + 1):
                    masked = jnp.where(label == g, right, 0.0).astype(BF16)
                    o = jnp.dot(rows_of, masked, preferred_element_type=F32)
                    t += o * o
                acc[r // rows : (r + 96) // rows] += t.reshape(96 // rows, rows, kg)
            return _

        lax.fori_loop(0, N, one, 0)

    acc[...] = jnp.zeros_like(acc)
    for b in range(2):
        owners(b)
    for b in range(2):
        contract(b)

    early = len(sends)

    mine = N * x + y
    for dy in range(N):
        for dz in range(N):
            yy, zz = up(y, dy), up(z, dz)
            send(
                acc.at[N * yy + zz],
                fr.at[mine],
                s_fr.at[mine],
                dev(held, yy, zz, c),
                when=None if dy or dz else jnp.logical_not(here),
            )

    @pl.when(here)
    def _():
        fr[mine] = acc[p]

    sent(sends[:early])
    t = jnp.zeros((rows, kg), F32)
    for dx in range(N):
        for dy in range(N):
            k = N * up(x, dx) + up(y, dy)
            if dx or dy:
                arrived(fr.at[k], s_fr.at[k])
            else:
                pl.when(jnp.logical_not(here))(lambda: arrived(fr.at[k], s_fr.at[k]))
    for k in range(N * N):
        t += fr[k]
    out[...] = t * (1.0 / (2 * 128 * SEQS))

    sent(sends[early:])


def per_device(activations, gradients, expert_ids, sequence_ids, input_basis, output_basis):
    micro, _, toks, wa = activations.shape
    wg = gradients.shape[3]
    pa, ka = input_basis.shape[1:]
    pgc, kg = output_basis.shape[1:]
    rows = ka // (N * N)
    vmem = pltpu.VMEM
    dma = pltpu.SemaphoreType.DMA
    anywhere = pl.BlockSpec(memory_space=pl.ANY)
    return pl.pallas_call(
        functools.partial(kernel, (toks, wa, wg, ka, kg, rows)),
        out_shape=jax.ShapeDtypeStruct((rows, kg), F32),
        in_specs=[pl.BlockSpec(memory_space=vmem)] * 2 + [anywhere] * 4,
        out_specs=pl.BlockSpec(memory_space=vmem),
        scratch_shapes=[
            vmem((8, 256), F32),
            vmem((8, 256), jnp.int32),
            vmem((2 * N, 8, 256), jnp.int32),
            vmem((2 * N, 8, 256), jnp.int32),
            vmem((2 * N, micro, toks, wg // N), BF16),
            vmem((2 * N, micro, toks, wa // N), BF16),
            vmem((N, N, pgc, kg), BF16),
            vmem((N, N, pa, ka), BF16),
            vmem((micro, N, N, PAIR, wg // N), BF16),
            vmem((micro, N, N, PAIR, wa // N), BF16),
            vmem((micro, N, N, PAIR, kg), BF16),
            vmem((micro, N, N, PAIR, ka), BF16),
            vmem((micro, N, N, PAIR, kg), BF16),
            vmem((micro, N, N, PAIR, ka), BF16),
            vmem((micro, N, PAIR, ka), BF16),
            vmem((micro, N, PAIR, ka), BF16),
            vmem((N * N, rows, kg), F32),
            vmem((N * N, rows, kg), F32),
            dma((256,)),
            dma((2 * N,)),
            dma((2 * N,)),
            dma((micro, 2 * N)),
            dma((micro, 2 * N)),
            dma((6,)),
            dma((3, N)),
            dma((3, 2)),
            dma((3, N, 4)),
            dma((micro, N)),
            dma((micro, N)),
            dma((micro, N)),
            dma((N * N,)),
        ],
        compiler_params=pltpu.CompilerParams(
            collective_id=0, has_side_effects=True, vmem_limit_bytes=63 << 20
        ),
        name="eigen",
    )(expert_ids[..., 0], sequence_ids, activations, gradients, input_basis, output_basis)[None]


def solution(mesh):
    placed = (
        P(None, ("expert", "panel"), None, None),
        P(None, ("expert", "panel"), None, None),
        P(None, ("expert", "panel"), None, None),
        P(None, ("expert", "panel"), None),
        P("expert", "panel", None),
        P("expert", "panel", None),
    )
    return jax.shard_map(
        per_device,
        mesh=mesh,
        in_specs=placed,
        out_specs=P("expert", "panel", None),
        check_vma=False,
    )
```

```python
import functools

import jax
import jax.numpy as jnp
from jax import lax
from jax.experimental import pallas as pl
from jax.experimental.pallas import tpu as pltpu
from jax.sharding import PartitionSpec as P

MESH = pl.DeviceIdType.MESH
SEQS = 4
N = 4
CAP = 18
PAIR = 48
NEAR = (0, 1, 3, 2)
TAG = 1024
BF16 = jnp.bfloat16
F32 = jnp.float32


def kernel(sizes, *refs):
    (ids, seqs, act, grad, ibs, gbs, out) = refs[:7]
    (lanes, codes, cz, cy, gx, ix, gb, ib, pg, pi, go, io, rg, ri, rs, ra, acc, fr) = refs[7:25]
    (s_send, s_cz, s_cy, s_gx, s_ix, s_loc, s_a, s_f, s_p, s_rg, s_ri, s_ra, s_fr) = refs[25:]
    toks, wa, wg, ka, kg, rows = sizes
    ga, gg = wa // N, wg // N
    pa, pgc = ga // N, gg // N
    e = lax.axis_index("expert")
    p = lax.axis_index("panel")
    x, c = e // 2, e % 2
    y, z = p // N, p % N
    other = 1 - c

    def dev(xx, yy, zz, cc):
        return (2 * xx + cc, N * yy + zz)

    def up(i, d):
        return (i + d) % N

    groups = {}

    def send(src, dst, sem, device, group, when=None):
        copy = pltpu.make_async_remote_copy(
            src_ref=src,
            dst_ref=dst,
            send_sem=s_send.at[groups.setdefault(group, len(groups))],
            recv_sem=sem,
            device_id=device,
            device_id_type=MESH,
        )
        if when is None:
            copy.start()
        else:
            pl.when(when)(lambda: copy.start())

    def sent(group, size):
        arrived(size, s_send.at[groups[group]])

    def arrived(ref, sem):
        pltpu.make_async_copy(ref, ref, sem).wait()

    held = up(z, N - x)
    here = x == held
    barrier = pltpu.get_barrier_semaphore()

    def greet(*device):
        pl.semaphore_signal(barrier, inc=1, device_id=dev(*device), device_id_type=MESH)

    xs, ys, zs = ([up(i, d) for d in range(N)] for i in (x, y, z))
    for d in range(1, N):
        greet(x, ys[d], z, other)
        greet(x, y, zs[d], other)
    greet(x, y, z, other)
    for dx in (2, 1, 3, 0):
        for dy in (2, 1, 3, 0):
            for dz in (2, 1, 3, 0):
                if dx or dy or dz:
                    greet(xs[dx], ys[dy], zs[dz], c)

    codes[...] = jnp.zeros_like(codes)
    lanes[...] = jnp.full_like(lanes, -1.0)
    above = lax.broadcasted_iota(jnp.int32, (2 * toks, 2 * toks), 0) < lax.broadcasted_iota(
        jnp.int32, (2 * toks, 2 * toks), 1
    )
    for b in range(2):
        for cc in range(2):

            @pl.when(c == cc)
            def _():
                lanes[b : b + 1, cc * toks : (cc + 1) * toks] = ids[b].astype(F32)

        row = lanes[b : b + 1, : 2 * toks]
        column = jnp.broadcast_to(row, (8, 2 * toks)).T[:, :1]
        earlier = jnp.logical_and(column == row, above)
        offset = jnp.sum(jnp.where(earlier, 1.0, 0.0), axis=0, keepdims=True).astype(jnp.int32)
        expert = row.astype(jnp.int32)
        number = (expert & 1) * TAG + (expert >> 1) * PAIR + offset + (1 + c * CAP)
        codes[b : b + 1, : 2 * toks] = jnp.where(expert < 0, 0, number)
    for cc in range(2):

        @pl.when(c == cc)
        def _():
            codes[2:4, cc * toks : (cc + 1) * toks] = seqs[:, 0] + (1 + SEQS * cc)

    pl.semaphore_wait(barrier, N * N * N + 2 * (N - 1))

    slot_z, slot_y = 2 * z + c, 2 * y + c
    for d in range(N):
        for cc in (c, other):
            if d == 0 and cc is c:
                continue
            send(codes, cz.at[slot_z], s_cz.at[slot_z], dev(x, y, up(z, d), cc), "cz")
            send(codes, cy.at[slot_y], s_cy.at[slot_y], dev(x, up(y, d), z, cc), "cy")

    cut = pgc // 2

    class Gather:
        def __init__(self, k, hbm, at, row, n, i1, i2, dev1, dev2, direct, buf):
            self.direct = direct
            self.parts = lambda a, b, r, n: buf.at[a, b, pl.ds(r, n)]
            self.k, self.at, self.row, self.n = k, at, row, n
            self.i1, self.i2, self.dev1, self.dev2 = i1, i2, dev1, dev2
            self.own = hbm.at[0, pl.ds(row, n)]

        def first(self):
            for d in (1, 3, 2) if self.direct else (1, 3):
                send(
                    self.own,
                    self.at(self.i1, self.i2, self.row, self.n),
                    s_a.at[self.k, self.i1],
                    self.dev1(up(self.i1, d)),
                    (self.k, 1),
                )

        def first_relay(self):
            h = self.n // 2
            for d, row in ((3, self.row), (1, self.row + h)):
                j = up(self.i1, d)
                arrived(self.at(j, self.i2, self.row, self.n), s_a.at[self.k, j])
                piece = self.at(j, self.i2, row, h)
                send(piece, piece, s_f.at[self.k, d // 2], self.dev1(up(self.i1, N - d)), (self.k, 1))

        def second(self, d):
            j = up(self.i1, d)
            land = self.at(j, self.i2, self.row, self.n)
            src = land if d else self.own
            if d and (self.direct or d != 2):
                if self.direct:
                    arrived(land, s_a.at[self.k, j])
            elif d:
                h = self.n // 2
                arrived(self.at(j, self.i2, self.row, h), s_f.at[self.k, 1])
                arrived(self.at(j, self.i2, self.row + h, h), s_f.at[self.k, 0])
            send(src, land, s_p.at[self.k, j, 0], self.dev2(up(self.i2, 1)), (self.k, 2))
            send(src, land, s_p.at[self.k, j, 1], self.dev2(up(self.i2, 3)), (self.k, 2))

        def relay(self, d):
            j = up(self.i1, d)
            h = self.n // 2
            left, right = up(self.i2, 3), up(self.i2, 1)
            arrived(self.at(j, left, self.row, self.n), s_p.at[self.k, j, 0])
            piece = self.at(j, left, self.row, h)
            send(piece, piece, s_p.at[self.k, j, 2], self.dev2(right), (self.k, 3))
            arrived(self.at(j, right, self.row, self.n), s_p.at[self.k, j, 1])
            piece = self.at(j, right, self.row + h, h)
            send(piece, piece, s_p.at[self.k, j, 3], self.dev2(left), (self.k, 3))

        def sent(self):
            sent((self.k, 1), self.parts(slice(0, 1), slice(0, 3), self.row, self.n))
            sent((self.k, 2), self.parts(slice(0, 2), slice(0, N), self.row, self.n))
            sent((self.k, 3), self.parts(slice(0, 1), slice(0, N), self.row, self.n))

        def last(self, d):
            j = up(self.i1, d)
            h = self.n // 2
            far = up(self.i2, 2)
            arrived(self.at(j, far, self.row, h), s_p.at[self.k, j, 2])
            arrived(self.at(j, far, self.row + h, h), s_p.at[self.k, j, 3])

    along_x = lambda j: dev(j, y, z, c)
    along_y = lambda j: dev(x, j, z, c)
    along_z = lambda j: dev(x, y, j, c)
    gb0 = Gather(
        0, gbs, lambda j1, j2, r, n: gb.at[j1, j2, pl.ds(r, n)], 0, cut, x, y, along_x, along_y, False, gb
    )
    gb1 = Gather(
        1, gbs, lambda j1, j2, r, n: gb.at[j2, j1, pl.ds(r, n)], cut, pgc - cut, y, x, along_y, along_x, False, gb
    )
    ibz = Gather(
        2, ibs, lambda j1, j2, r, n: ib.at[j2, j1, pl.ds(r, n)], 0, pa, z, x, along_z, along_x, True, ib
    )

    gb0.first()
    gb1.first()
    ibz.first()

    def grad_part(b, zz, k):
        return grad.at[b, 0, :, pl.ds(pl.multiple_of((k * N + zz) * pgc, pgc), pgc)]

    def act_part(b, yy):
        return act.at[b, 0, :, pl.ds(pl.multiple_of(yy * ga, ga), ga)]

    def gx_part(b, k):
        return gx.at[slot_z, b, :, pl.ds(k * pgc, pgc)]

    def send_grad(b, d):
        for k in range(N):
            send(
                grad_part(b, up(z, d), k),
                gx_part(b, k),
                s_gx.at[b, slot_z],
                along_z(up(z, d)),
                ("grad", b),
            )

    def send_act(b, d):
        send(act_part(b, up(y, d)), ix.at[slot_y, b], s_ix.at[b, slot_y], along_y(up(y, d)), ("act", b))

    def own_rows(b):
        for k in range(N):
            pltpu.make_async_copy(grad_part(b, z, k), gx_part(b, k), s_loc.at[b]).start()
            send(
                grad_part(b, z, k),
                gx_part(b, k),
                s_gx.at[b, slot_z],
                dev(x, y, z, other),
                ("grad", b),
            )
        pltpu.make_async_copy(act_part(b, y), ix.at[slot_y, b], s_loc.at[2 + b]).start()
        send(
            act_part(b, y), ix.at[slot_y, b], s_ix.at[b, slot_y], dev(x, y, z, other), ("act", b)
        )

    for d in (1, 3, 2):
        send_grad(0, d)
    ibz.second(0)
    gb0.second(0)
    gb0.first_relay()
    gb1.first_relay()
    for d in (1, 3, 2):
        send_act(0, d)
    gb1.second(0)
    own_rows(0)
    pltpu.make_async_copy(gbs.at[0], gb.at[x, y], s_loc.at[4]).start()
    pltpu.make_async_copy(ibs.at[0], ib.at[x, z], s_loc.at[5]).start()
    cz[slot_z] = codes[...]
    cy[slot_y] = codes[...]
    for d in (1, 3, 2):
        send_grad(1, d)
    own_rows(1)

    for d in (1, 3, 2):
        ibz.second(d)
        gb0.second(d)
    for d in (1, 3, 2):
        gb1.second(d)
    for d in (1, 3, 2):
        send_act(1, d)

    for d in range(N):
        for cc in (c, other):
            if d == 0 and cc is c:
                continue
            sz, sy = 2 * up(z, d) + cc, 2 * up(y, d) + cc
            arrived(cz.at[sz], s_cz.at[sz])
            arrived(cy.at[sy], s_cy.at[sy])

    def hand_on(buf, sem, b, q):
        s = 2 * q + c
        arrived(buf.at[s, b], sem.at[b, s])
        group = ("on", buf is gx, b)
        send(buf.at[s, b], buf.at[s, b], sem.at[b, s], dev(x, y, z, other), group)

    slots = N * PAIR

    def pack(buf, sem, code, dst, b, q, pos, chunk):
        s = 2 * q + other
        arrived(buf.at[s, b], sem.at[b, s])
        numbers = code[2 * q, b : b + 1, : 2 * toks] + code[2 * q + 1, b : b + 1, : 2 * toks]
        mine = lax.broadcasted_iota(jnp.int32, (slots, 2 * toks), 0) + (1 + c * TAG)
        place = jnp.where(numbers == mine, 1.0, 0.0).astype(BF16)

        def step(i, _):
            cols = pl.ds(pl.multiple_of(i * chunk, chunk), chunk)
            block = buf[pl.ds(2 * q, 2), b, :, cols].reshape(2 * toks, chunk)
            packed = jnp.dot(place, block, preferred_element_type=F32).astype(BF16)
            dst[b, :, pos, :, cols] = packed.reshape(N, PAIR, chunk)
            return _

        lax.fori_loop(0, buf.shape[3] // chunk, step, 0)

    def pack_grad(b, d):
        pack(gx, s_gx, cz, pg, b, up(z, d), NEAR.index(d), 512)

    def pack_act(b, d):
        pack(ix, s_ix, cy, pi, b, up(y, d), NEAR.index(d), 512)

    def local_rows(b):
        for k in range(N):
            arrived(gx_part(b, k), s_loc.at[b])
        arrived(ix.at[slot_y, b], s_loc.at[2 + b])

    def rotate(src, basis, dst, b, k, lo, hi):
        depth = basis.shape[2]
        m = (hi - lo) * PAIR
        t = jnp.zeros((m, basis.shape[3]), F32)
        for j in range(N):
            block = src[b, k, lo:hi, :, j * depth : (j + 1) * depth].reshape(m, depth)
            t += jnp.dot(block, basis[k, j], preferred_element_type=F32)
        dst[b, k, lo:hi] = t.astype(BF16).reshape(hi - lo, PAIR, basis.shape[3])

    def rotate_in(b, experts):
        for d in experts:
            rotate(pi, ib, io, b, up(x, d), 0, N)

    def rotate_out(b, experts, lo, hi):
        for d in experts:
            rotate(pg, gb, go, b, up(x, d), lo, hi)

    def share(src, dst, sem, me, along, b, experts, lo, hi):
        for d in experts:
            k = up(x, d)
            owner = (k + x) % N
            for i in range(lo, hi):
                send(
                    src.at[b, k, i],
                    dst.at[b, me, up(me, NEAR[i])],
                    sem.at[b, me],
                    along(owner),
                    ("share", src is io, b),
                    when=owner != me,
                )

    def share_in(b, experts):
        share(io, ri, s_ri, y, along_y, b, experts, 0, N)

    def share_out(b, experts, lo, hi):
        share(go, rg, s_rg, z, along_z, b, experts, lo, hi)

    close, far = NEAR[:3], NEAR[3:]

    local_rows(0)
    for d in (1, 3, 2):
        hand_on(ix, s_ix, 0, up(y, d))
    for d in (1, 3):
        hand_on(gx, s_gx, 0, up(z, d))
    for d in NEAR:
        pack_act(0, d)
    arrived(ib.at[x, z], s_loc.at[5])
    for d in close:
        pack_grad(0, d)
    for d in NEAR:
        ibz.relay(d)
    rotate_in(0, close)
    share_in(0, close)
    hand_on(gx, s_gx, 0, up(z, 2))
    for d in NEAR:
        gb0.relay(d)
    pack_grad(0, 2)
    local_rows(1)
    for d in (1, 3, 2):
        hand_on(ix, s_ix, 1, up(y, d))
    for d in NEAR:
        gb1.relay(d)
    for d in NEAR:
        pack_act(1, d)
    rotate_in(1, close)
    share_in(1, close)
    for d in (1, 3):
        hand_on(gx, s_gx, 1, up(z, d))
    for d in close:
        pack_grad(1, d)
    for d in NEAR:
        ibz.last(d)
    for b in range(2):
        rotate_in(b, far)
        share_in(b, far)
    arrived(gb.at[x, y], s_loc.at[4])
    for d in close:
        gb0.last(d)
        rotate_out(0, (d,), 0, N)
        rotate_out(1, (d,), 0, 3)
        share_out(0, (d,), 0, N)
        share_out(1, (d,), 0, 3)
    gb0.last(2)
    for d in range(N):
        gb1.last(d)
    rotate_out(0, far, 0, N)
    rotate_out(1, far, 0, 3)
    share_out(0, far, 0, N)
    share_out(1, far, 0, 3)
    hand_on(gx, s_gx, 1, up(z, 2))
    pack_grad(1, 2)
    rotate_out(1, NEAR, 3, N)
    share_out(1, NEAR, 3, N)

    def owned(src, dst, sem, me, b, store):
        for d in (1, 3, 2):
            k = up(me, d)
            arrived(dst.at[b, k], sem.at[b, k])
        for i, d in enumerate(NEAR):
            q = up(me, d)
            t = src[b, up(me, N - x), i].astype(F32)
            for j in (1, 3, 2):
                t += dst[b, up(me, j), q].astype(F32)
            store(q, t.astype(BF16))

    stays = y == z

    def owners(b):
        def store(q, value):
            rs[b, q] = value

        owned(io, ri, s_ri, y, b, store)
        for d in (1, 3, 2, 0):
            k = up(y, d)
            send(
                rs.at[b, k],
                ra.at[b, z],
                s_ra.at[b, z],
                dev(x, k, y, c),
                ("own", b, d == 0),
                when=None if d else jnp.logical_not(stays),
            )

        @pl.when(stays)
        def _():
            ra[b, z] = rs[b, y]

    def contract(b):
        def store(q, value):
            rg[b, z, q] = value

        owned(go, rg, s_rg, z, b, store)
        for d in range(N):
            k = up(z, d)
            if d == 0:
                pl.when(jnp.logical_not(stays))(lambda: arrived(ra.at[b, k], s_ra.at[b, k]))
            else:
                arrived(ra.at[b, k], s_ra.at[b, k])

        def one(k, _):
            numbers = cz[2 * k, b : b + 1, : 2 * toks] + cz[2 * k + 1, b : b + 1, : 2 * toks]
            labels = (
                cz[2 * k, 2 + b : 3 + b, : 2 * toks] + cz[2 * k + 1, 2 + b : 3 + b, : 2 * toks]
            )
            mine = lax.broadcasted_iota(jnp.int32, (PAIR, 2 * toks), 0) + (
                1 + c * TAG + up(z, N - x) * PAIR
            )
            label = jnp.sum(jnp.where(numbers == mine, labels, 0), axis=1, keepdims=True)
            left = ra[b, k].astype(F32).T.astype(BF16)
            right = rg[b, z, k].astype(F32)
            for r in range(0, ka, 96):
                rows_of = left[r : r + 96]
                t = jnp.zeros((96, kg), F32)
                for g in range(1, 2 * SEQS + 1):
                    masked = jnp.where(label == g, right, 0.0).astype(BF16)
                    o = jnp.dot(rows_of, masked, preferred_element_type=F32)
                    t += o * o
                acc[r // rows : (r + 96) // rows] += t.reshape(96 // rows, rows, kg)
            return _

        lax.fori_loop(0, N, one, 0)

    acc[...] = jnp.zeros_like(acc)
    for b in range(2):
        owners(b)
    for b in range(2):
        contract(b)

    mine = N * x + y
    for dy in range(N):
        for dz in range(N):
            yy, zz = up(y, dy), up(z, dz)
            send(
                acc.at[N * yy + zz],
                fr.at[mine],
                s_fr.at[mine],
                dev(held, yy, zz, c),
                ("sums", not (dy or dz)),
                when=None if dy or dz else jnp.logical_not(here),
            )

    @pl.when(here)
    def _():
        fr[mine] = acc[p]

    sent("cz", cz.at[pl.ds(0, 2 * N - 1)])
    sent("cy", cy.at[pl.ds(0, 2 * N - 1)])
    gb0.sent()
    gb1.sent()
    ibz.sent()
    for b in range(2):
        sent(("grad", b), gx.at[pl.ds(0, N), b])
        sent(("act", b), ix.at[pl.ds(0, N), b])
        sent(("on", True, b), gx.at[pl.ds(0, N - 1), b])
        sent(("on", False, b), ix.at[pl.ds(0, N - 1), b])
        sent(("share", True, b), ri.at[b, pl.ds(0, N - 1)])
        sent(("share", False, b), rg.at[b, pl.ds(0, N - 1)])
        sent(("own", b, False), ra.at[b, pl.ds(0, N - 1)])
        pl.when(jnp.logical_not(stays))(lambda: sent(("own", b, True), ra.at[b, 0]))
    t = jnp.zeros((rows, kg), F32)
    for dx in range(N):
        for dy in range(N):
            k = N * up(x, dx) + up(y, dy)
            if dx or dy:
                arrived(fr.at[k], s_fr.at[k])
            else:
                pl.when(jnp.logical_not(here))(lambda: arrived(fr.at[k], s_fr.at[k]))
    for k in range(N * N):
        t += fr[k]
    out[...] = t * (1.0 / (2 * 128 * SEQS))

    sent(("sums", False), fr.at[pl.ds(0, N * N - 1)])
    pl.when(jnp.logical_not(here))(lambda: sent(("sums", True), fr.at[0]))


def per_device(activations, gradients, expert_ids, sequence_ids, input_basis, output_basis):
    micro, _, toks, wa = activations.shape
    wg = gradients.shape[3]
    pa, ka = input_basis.shape[1:]
    pgc, kg = output_basis.shape[1:]
    rows = ka // (N * N)
    vmem = pltpu.VMEM
    dma = pltpu.SemaphoreType.DMA
    anywhere = pl.BlockSpec(memory_space=pl.ANY)
    return pl.pallas_call(
        functools.partial(kernel, (toks, wa, wg, ka, kg, rows)),
        out_shape=jax.ShapeDtypeStruct((rows, kg), F32),
        in_specs=[pl.BlockSpec(memory_space=vmem)] * 2 + [anywhere] * 4,
        out_specs=pl.BlockSpec(memory_space=vmem),
        scratch_shapes=[
            vmem((8, 256), F32),
            vmem((8, 256), jnp.int32),
            vmem((2 * N, 8, 256), jnp.int32),
            vmem((2 * N, 8, 256), jnp.int32),
            vmem((2 * N, micro, toks, wg // N), BF16),
            vmem((2 * N, micro, toks, wa // N), BF16),
            vmem((N, N, pgc, kg), BF16),
            vmem((N, N, pa, ka), BF16),
            vmem((micro, N, N, PAIR, wg // N), BF16),
            vmem((micro, N, N, PAIR, wa // N), BF16),
            vmem((micro, N, N, PAIR, kg), BF16),
            vmem((micro, N, N, PAIR, ka), BF16),
            vmem((micro, N, N, PAIR, kg), BF16),
            vmem((micro, N, N, PAIR, ka), BF16),
            vmem((micro, N, PAIR, ka), BF16),
            vmem((micro, N, PAIR, ka), BF16),
            vmem((N * N, rows, kg), F32),
            vmem((N * N, rows, kg), F32),
            dma((32,)),
            dma((2 * N,)),
            dma((2 * N,)),
            dma((micro, 2 * N)),
            dma((micro, 2 * N)),
            dma((6,)),
            dma((3, N)),
            dma((3, 2)),
            dma((3, N, 4)),
            dma((micro, N)),
            dma((micro, N)),
            dma((micro, N)),
            dma((N * N,)),
        ],
        compiler_params=pltpu.CompilerParams(
            collective_id=0, has_side_effects=True, vmem_limit_bytes=63 << 20
        ),
        name="eigen",
    )(expert_ids[..., 0], sequence_ids, activations, gradients, input_basis, output_basis)[None]


def solution(mesh):
    placed = (
        P(None, ("expert", "panel"), None, None),
        P(None, ("expert", "panel"), None, None),
        P(None, ("expert", "panel"), None, None),
        P(None, ("expert", "panel"), None),
        P("expert", "panel", None),
        P("expert", "panel", None),
    )
    return jax.shard_map(
        per_device,
        mesh=mesh,
        in_specs=placed,
        out_specs=P("expert", "panel", None),
        check_vma=False,
    )
```

```python
import functools

import jax
import jax.numpy as jnp
from jax import lax
from jax.experimental import pallas as pl
from jax.experimental.pallas import tpu as pltpu
from jax.sharding import PartitionSpec as P

MESH = pl.DeviceIdType.MESH
SEQS = 4
N = 4
CAP = 18
USED = 40
PAIR = 48
NEAR = (0, 1, 3, 2)
TAG = 1024
BF16 = jnp.bfloat16
F32 = jnp.float32


def kernel(sizes, *refs):
    (ids, seqs, act, grad, ibs, gbs, out) = refs[:7]
    (lanes, codes, cz, cy, gx, ix, gb, ib, pg, pi, go, io, rg, ri, rs, ra, acc, fr) = refs[7:25]
    (s_send, s_cz, s_cy, s_gx, s_ix, s_loc, s_a, s_f, s_p, s_rg, s_ri, s_ra, s_fr) = refs[25:]
    toks, wa, wg, ka, kg, rows = sizes
    ga, gg = wa // N, wg // N
    pa, pgc = ga // N, gg // N
    e = lax.axis_index("expert")
    p = lax.axis_index("panel")
    x, c = e // 2, e % 2
    y, z = p // N, p % N
    other = 1 - c

    def dev(xx, yy, zz, cc):
        return (2 * xx + cc, N * yy + zz)

    def up(i, d):
        return (i + d) % N

    groups = {}

    def send(src, dst, sem, device, group, when=None):
        copy = pltpu.make_async_remote_copy(
            src_ref=src,
            dst_ref=dst,
            send_sem=s_send.at[groups.setdefault(group, len(groups))],
            recv_sem=sem,
            device_id=device,
            device_id_type=MESH,
        )
        if when is None:
            copy.start()
        else:
            pl.when(when)(lambda: copy.start())

    def sent(group, size):
        arrived(size, s_send.at[groups[group]])

    def arrived(ref, sem):
        pltpu.make_async_copy(ref, ref, sem).wait()

    held = up(z, N - x)
    here = x == held
    barrier = pltpu.get_barrier_semaphore()

    def greet(*device):
        pl.semaphore_signal(barrier, inc=1, device_id=dev(*device), device_id_type=MESH)

    xs, ys, zs = ([up(i, d) for d in range(N)] for i in (x, y, z))
    for d in range(1, N):
        greet(x, ys[d], z, other)
        greet(x, y, zs[d], other)
    greet(x, y, z, other)
    for dx in (2, 1, 3, 0):
        for dy in (2, 1, 3, 0):
            for dz in (2, 1, 3, 0):
                if dx or dy or dz:
                    greet(xs[dx], ys[dy], zs[dz], c)

    codes[...] = jnp.zeros_like(codes)
    lanes[...] = jnp.full_like(lanes, -1.0)
    above = lax.broadcasted_iota(jnp.int32, (2 * toks, 2 * toks), 0) < lax.broadcasted_iota(
        jnp.int32, (2 * toks, 2 * toks), 1
    )
    for b in range(2):
        for cc in range(2):

            @pl.when(c == cc)
            def _():
                lanes[b : b + 1, cc * toks : (cc + 1) * toks] = ids[b].astype(F32)

        row = lanes[b : b + 1, : 2 * toks]
        column = jnp.broadcast_to(row, (8, 2 * toks)).T[:, :1]
        earlier = jnp.logical_and(column == row, above)
        offset = jnp.sum(jnp.where(earlier, 1.0, 0.0), axis=0, keepdims=True).astype(jnp.int32)
        expert = row.astype(jnp.int32)
        number = (expert & 1) * TAG + (expert >> 1) * PAIR + offset + (1 + c * CAP)
        codes[b : b + 1, : 2 * toks] = jnp.where(expert < 0, 0, number)
    for cc in range(2):

        @pl.when(c == cc)
        def _():
            codes[2:4, cc * toks : (cc + 1) * toks] = seqs[:, 0] + (1 + SEQS * cc)

    pl.semaphore_wait(barrier, N * N * N + 2 * (N - 1))

    slot_z, slot_y = 2 * z + c, 2 * y + c
    for d in range(N):
        for cc in (c, other):
            if d == 0 and cc is c:
                continue
            send(codes, cz.at[slot_z], s_cz.at[slot_z], dev(x, y, up(z, d), cc), "cz")
            send(codes, cy.at[slot_y], s_cy.at[slot_y], dev(x, up(y, d), z, cc), "cy")

    cut = pgc // 2

    class Gather:
        def __init__(self, k, hbm, at, row, n, i1, i2, dev1, dev2, direct, buf):
            self.direct = direct
            self.parts = lambda a, b, r, n: buf.at[a, b, pl.ds(r, n)]
            self.k, self.at, self.row, self.n = k, at, row, n
            self.i1, self.i2, self.dev1, self.dev2 = i1, i2, dev1, dev2
            self.own = hbm.at[0, pl.ds(row, n)]

        def first(self):
            for d in (1, 3, 2) if self.direct else (1, 3):
                send(
                    self.own,
                    self.at(self.i1, self.i2, self.row, self.n),
                    s_a.at[self.k, self.i1],
                    self.dev1(up(self.i1, d)),
                    (self.k, 1),
                )

        def first_relay(self):
            h = self.n // 2
            for d, row in ((3, self.row), (1, self.row + h)):
                j = up(self.i1, d)
                arrived(self.at(j, self.i2, self.row, self.n), s_a.at[self.k, j])
                piece = self.at(j, self.i2, row, h)
                send(piece, piece, s_f.at[self.k, d // 2], self.dev1(up(self.i1, N - d)), (self.k, 1))

        def second(self, d):
            j = up(self.i1, d)
            land = self.at(j, self.i2, self.row, self.n)
            src = land if d else self.own
            if d and (self.direct or d != 2):
                if self.direct:
                    arrived(land, s_a.at[self.k, j])
            elif d:
                h = self.n // 2
                arrived(self.at(j, self.i2, self.row, h), s_f.at[self.k, 1])
                arrived(self.at(j, self.i2, self.row + h, h), s_f.at[self.k, 0])
            send(src, land, s_p.at[self.k, j, 0], self.dev2(up(self.i2, 1)), (self.k, 2))
            send(src, land, s_p.at[self.k, j, 1], self.dev2(up(self.i2, 3)), (self.k, 2))

        def relay(self, d):
            j = up(self.i1, d)
            h = self.n // 2
            left, right = up(self.i2, 3), up(self.i2, 1)
            arrived(self.at(j, left, self.row, self.n), s_p.at[self.k, j, 0])
            piece = self.at(j, left, self.row, h)
            send(piece, piece, s_p.at[self.k, j, 2], self.dev2(right), (self.k, 3))
            arrived(self.at(j, right, self.row, self.n), s_p.at[self.k, j, 1])
            piece = self.at(j, right, self.row + h, h)
            send(piece, piece, s_p.at[self.k, j, 3], self.dev2(left), (self.k, 3))

        def sent(self):
            sent((self.k, 1), self.parts(slice(0, 1), slice(0, 3), self.row, self.n))
            sent((self.k, 2), self.parts(slice(0, 2), slice(0, N), self.row, self.n))
            sent((self.k, 3), self.parts(slice(0, 1), slice(0, N), self.row, self.n))

        def last(self, d):
            j = up(self.i1, d)
            h = self.n // 2
            far = up(self.i2, 2)
            arrived(self.at(j, far, self.row, h), s_p.at[self.k, j, 2])
            arrived(self.at(j, far, self.row + h, h), s_p.at[self.k, j, 3])

    along_x = lambda j: dev(j, y, z, c)
    along_y = lambda j: dev(x, j, z, c)
    along_z = lambda j: dev(x, y, j, c)
    gb0 = Gather(
        0, gbs, lambda j1, j2, r, n: gb.at[j1, j2, pl.ds(r, n)], 0, cut, x, y, along_x, along_y, False, gb
    )
    gb1 = Gather(
        1, gbs, lambda j1, j2, r, n: gb.at[j2, j1, pl.ds(r, n)], cut, pgc - cut, y, x, along_y, along_x, False, gb
    )
    ibz = Gather(
        2, ibs, lambda j1, j2, r, n: ib.at[j2, j1, pl.ds(r, n)], 0, pa, z, x, along_z, along_x, True, ib
    )

    gb0.first()
    gb1.first()
    ibz.first()

    def grad_part(b, zz, k):
        return grad.at[b, 0, :, pl.ds(pl.multiple_of((k * N + zz) * pgc, pgc), pgc)]

    def act_part(b, yy):
        return act.at[b, 0, :, pl.ds(pl.multiple_of(yy * ga, ga), ga)]

    def gx_part(b, k):
        return gx.at[slot_z, b, :, pl.ds(k * pgc, pgc)]

    def send_grad(b, d):
        for k in range(N):
            send(
                grad_part(b, up(z, d), k),
                gx_part(b, k),
                s_gx.at[b, slot_z],
                along_z(up(z, d)),
                ("grad", b),
            )

    def send_act(b, d):
        send(act_part(b, up(y, d)), ix.at[slot_y, b], s_ix.at[b, slot_y], along_y(up(y, d)), ("act", b))

    def own_rows(b):
        for k in range(N):
            pltpu.make_async_copy(grad_part(b, z, k), gx_part(b, k), s_loc.at[b]).start()
            send(
                grad_part(b, z, k),
                gx_part(b, k),
                s_gx.at[b, slot_z],
                dev(x, y, z, other),
                ("grad", b),
            )
        pltpu.make_async_copy(act_part(b, y), ix.at[slot_y, b], s_loc.at[2 + b]).start()
        send(
            act_part(b, y), ix.at[slot_y, b], s_ix.at[b, slot_y], dev(x, y, z, other), ("act", b)
        )

    for d in (1, 3, 2):
        send_grad(0, d)
    ibz.second(0)
    gb0.second(0)
    gb0.first_relay()
    gb1.first_relay()
    for d in (1, 3, 2):
        send_act(0, d)
    gb1.second(0)
    own_rows(0)
    pltpu.make_async_copy(gbs.at[0], gb.at[x, y], s_loc.at[4]).start()
    pltpu.make_async_copy(ibs.at[0], ib.at[x, z], s_loc.at[5]).start()
    cz[slot_z] = codes[...]
    cy[slot_y] = codes[...]
    for d in (1, 3, 2):
        send_grad(1, d)
    own_rows(1)

    for d in (1, 3, 2):
        ibz.second(d)
        gb0.second(d)
    for d in (1, 3, 2):
        gb1.second(d)
    for d in (1, 3, 2):
        send_act(1, d)

    for d in range(N):
        for cc in (c, other):
            if d == 0 and cc is c:
                continue
            sz, sy = 2 * up(z, d) + cc, 2 * up(y, d) + cc
            arrived(cz.at[sz], s_cz.at[sz])
            arrived(cy.at[sy], s_cy.at[sy])

    def hand_on(buf, sem, b, q):
        s = 2 * q + c
        arrived(buf.at[s, b], sem.at[b, s])
        group = ("on", buf is gx, b)
        send(buf.at[s, b], buf.at[s, b], sem.at[b, s], dev(x, y, z, other), group)

    slots = N * PAIR

    def pack(buf, sem, code, dst, b, q, pos, chunk):
        s = 2 * q + other
        arrived(buf.at[s, b], sem.at[b, s])
        numbers = code[2 * q, b : b + 1, : 2 * toks] + code[2 * q + 1, b : b + 1, : 2 * toks]
        mine = lax.broadcasted_iota(jnp.int32, (slots, 2 * toks), 0) + (1 + c * TAG)
        place = jnp.where(numbers == mine, 1.0, 0.0).astype(BF16)

        def step(i, _):
            cols = pl.ds(pl.multiple_of(i * chunk, chunk), chunk)
            block = buf[pl.ds(2 * q, 2), b, :, cols].reshape(2 * toks, chunk)
            packed = jnp.dot(place, block, preferred_element_type=F32).astype(BF16)
            dst[b, :, pos, :, cols] = packed.reshape(N, PAIR, chunk)
            return _

        lax.fori_loop(0, buf.shape[3] // chunk, step, 0)

    def pack_grad(b, d):
        pack(gx, s_gx, cz, pg, b, up(z, d), NEAR.index(d), 512)

    def pack_act(b, d):
        pack(ix, s_ix, cy, pi, b, up(y, d), NEAR.index(d), 512)

    def local_rows(b):
        for k in range(N):
            arrived(gx_part(b, k), s_loc.at[b])
        arrived(ix.at[slot_y, b], s_loc.at[2 + b])

    def rotate(src, basis, dst, b, k, lo, hi):
        depth = basis.shape[2]
        m = (hi - lo) * PAIR
        t = jnp.zeros((m, basis.shape[3]), F32)
        for j in range(N):
            block = src[b, k, lo:hi, :, j * depth : (j + 1) * depth].reshape(m, depth)
            t += jnp.dot(block, basis[k, j], preferred_element_type=F32)
        dst[b, k, lo:hi] = t.astype(BF16).reshape(hi - lo, PAIR, basis.shape[3])

    def rotate_in(b, experts):
        for d in experts:
            rotate(pi, ib, io, b, up(x, d), 0, N)

    def rotate_out(b, experts, lo, hi):
        for d in experts:
            rotate(pg, gb, go, b, up(x, d), lo, hi)

    def share(src, dst, sem, me, along, b, experts, lo, hi):
        for d in experts:
            k = up(x, d)
            owner = (k + x) % N
            for i in range(lo, hi):
                send(
                    src.at[b, k, i, pl.ds(0, USED)],
                    dst.at[b, me, up(me, NEAR[i]), pl.ds(0, USED)],
                    sem.at[b, me],
                    along(owner),
                    ("share", src is io, b),
                    when=owner != me,
                )

    def share_in(b, experts):
        share(io, ri, s_ri, y, along_y, b, experts, 0, N)

    def share_out(b, experts, lo, hi):
        share(go, rg, s_rg, z, along_z, b, experts, lo, hi)

    close, far = NEAR[:3], NEAR[3:]

    local_rows(0)
    for d in (1, 3, 2):
        hand_on(ix, s_ix, 0, up(y, d))
    for d in (1, 3):
        hand_on(gx, s_gx, 0, up(z, d))
    for d in NEAR:
        ibz.relay(d)
    for d in NEAR:
        pack_act(0, d)
    arrived(ib.at[x, z], s_loc.at[5])
    for d in NEAR:
        gb0.relay(d)
    for d in close:
        pack_grad(0, d)
    rotate_in(0, close)
    share_in(0, close)
    hand_on(gx, s_gx, 0, up(z, 2))
    for d in NEAR:
        gb1.relay(d)
    pack_grad(0, 2)
    local_rows(1)
    for d in (1, 3, 2):
        hand_on(ix, s_ix, 1, up(y, d))
    for d in NEAR:
        pack_act(1, d)
    rotate_in(1, close)
    share_in(1, close)
    for d in (1, 3):
        hand_on(gx, s_gx, 1, up(z, d))
    for d in close:
        pack_grad(1, d)
    for d in NEAR:
        ibz.last(d)
    for b in range(2):
        rotate_in(b, far)
        share_in(b, far)
    arrived(gb.at[x, y], s_loc.at[4])
    for d in close:
        gb0.last(d)
        rotate_out(0, (d,), 0, N)
        rotate_out(1, (d,), 0, 3)
        share_out(0, (d,), 0, N)
        share_out(1, (d,), 0, 3)
    gb0.last(2)
    for d in range(N):
        gb1.last(d)
    rotate_out(0, far, 0, N)
    rotate_out(1, far, 0, 3)
    share_out(0, far, 0, N)
    share_out(1, far, 0, 3)
    hand_on(gx, s_gx, 1, up(z, 2))
    pack_grad(1, 2)
    rotate_out(1, NEAR, 3, N)
    share_out(1, NEAR, 3, N)

    def owned(src, dst, sem, me, b, store):
        for d in (1, 3, 2):
            k = up(me, d)
            arrived(dst.at[b, k, :, pl.ds(0, USED)], sem.at[b, k])
        for i, d in enumerate(NEAR):
            q = up(me, d)
            t = src[b, up(me, N - x), i, :USED].astype(F32)
            for j in (1, 3, 2):
                t += dst[b, up(me, j), q, :USED].astype(F32)
            store(q, t.astype(BF16))

    stays = y == z

    def owners(b):
        def store(q, value):
            rs[b, q, :USED] = value

        owned(io, ri, s_ri, y, b, store)
        for d in (1, 3, 2, 0):
            k = up(y, d)
            send(
                rs.at[b, k, pl.ds(0, USED)],
                ra.at[b, z, pl.ds(0, USED)],
                s_ra.at[b, z],
                dev(x, k, y, c),
                ("own", b, d == 0),
                when=None if d else jnp.logical_not(stays),
            )

        @pl.when(stays)
        def _():
            ra[b, z, :USED] = rs[b, y, :USED]

    def contract(b):
        def store(q, value):
            rg[b, z, q, :USED] = value

        owned(go, rg, s_rg, z, b, store)
        for d in range(N):
            k = up(z, d)
            if d == 0:
                pl.when(jnp.logical_not(stays))(lambda: arrived(ra.at[b, k, pl.ds(0, USED)], s_ra.at[b, k]))
            else:
                arrived(ra.at[b, k, pl.ds(0, USED)], s_ra.at[b, k])

        def one(k, _):
            numbers = cz[2 * k, b : b + 1, : 2 * toks] + cz[2 * k + 1, b : b + 1, : 2 * toks]
            labels = (
                cz[2 * k, 2 + b : 3 + b, : 2 * toks] + cz[2 * k + 1, 2 + b : 3 + b, : 2 * toks]
            )
            mine = lax.broadcasted_iota(jnp.int32, (USED, 2 * toks), 0) + (
                1 + c * TAG + up(z, N - x) * PAIR
            )
            label = jnp.sum(jnp.where(numbers == mine, labels, 0), axis=1, keepdims=True)
            left = ra[b, k, :USED].astype(F32).T.astype(BF16)
            right = rg[b, z, k, :USED].astype(F32)
            for r in range(0, ka, 96):
                rows_of = left[r : r + 96]
                t = jnp.zeros((96, kg), F32)
                for g in range(1, 2 * SEQS + 1):
                    masked = jnp.where(label == g, right, 0.0).astype(BF16)
                    o = jnp.dot(rows_of, masked, preferred_element_type=F32)
                    t += o * o
                acc[r // rows : (r + 96) // rows] += t.reshape(96 // rows, rows, kg)
            return _

        lax.fori_loop(0, N, one, 0)

    acc[...] = jnp.zeros_like(acc)
    for b in range(2):
        owners(b)
    for b in range(2):
        contract(b)

    mine = N * x + y
    for dy in range(N):
        for dz in range(N):
            yy, zz = up(y, dy), up(z, dz)
            send(
                acc.at[N * yy + zz],
                fr.at[mine],
                s_fr.at[mine],
                dev(held, yy, zz, c),
                ("sums", not (dy or dz)),
                when=None if dy or dz else jnp.logical_not(here),
            )

    @pl.when(here)
    def _():
        fr[mine] = acc[p]

    sent("cz", cz.at[pl.ds(0, 2 * N - 1)])
    sent("cy", cy.at[pl.ds(0, 2 * N - 1)])
    gb0.sent()
    gb1.sent()
    ibz.sent()
    for b in range(2):
        sent(("grad", b), gx.at[pl.ds(0, N), b])
        sent(("act", b), ix.at[pl.ds(0, N), b])
        sent(("on", True, b), gx.at[pl.ds(0, N - 1), b])
        sent(("on", False, b), ix.at[pl.ds(0, N - 1), b])
        sent(("share", True, b), ri.at[b, pl.ds(0, N - 1), :, pl.ds(0, USED)])
        sent(("share", False, b), rg.at[b, pl.ds(0, N - 1), :, pl.ds(0, USED)])
        sent(("own", b, False), ra.at[b, pl.ds(0, N - 1), pl.ds(0, USED)])
        pl.when(jnp.logical_not(stays))(lambda: sent(("own", b, True), ra.at[b, 0, pl.ds(0, USED)]))
    t = jnp.zeros((rows, kg), F32)
    for dx in range(N):
        for dy in range(N):
            k = N * up(x, dx) + up(y, dy)
            if dx or dy:
                arrived(fr.at[k], s_fr.at[k])
            else:
                pl.when(jnp.logical_not(here))(lambda: arrived(fr.at[k], s_fr.at[k]))
    for k in range(N * N):
        t += fr[k]
    out[...] = t * (1.0 / (2 * 128 * SEQS))

    sent(("sums", False), fr.at[pl.ds(0, N * N - 1)])
    pl.when(jnp.logical_not(here))(lambda: sent(("sums", True), fr.at[0]))


def per_device(activations, gradients, expert_ids, sequence_ids, input_basis, output_basis):
    micro, _, toks, wa = activations.shape
    wg = gradients.shape[3]
    pa, ka = input_basis.shape[1:]
    pgc, kg = output_basis.shape[1:]
    rows = ka // (N * N)
    vmem = pltpu.VMEM
    dma = pltpu.SemaphoreType.DMA
    anywhere = pl.BlockSpec(memory_space=pl.ANY)
    return pl.pallas_call(
        functools.partial(kernel, (toks, wa, wg, ka, kg, rows)),
        out_shape=jax.ShapeDtypeStruct((rows, kg), F32),
        in_specs=[pl.BlockSpec(memory_space=vmem)] * 2 + [anywhere] * 4,
        out_specs=pl.BlockSpec(memory_space=vmem),
        scratch_shapes=[
            vmem((8, 256), F32),
            vmem((8, 256), jnp.int32),
            vmem((2 * N, 8, 256), jnp.int32),
            vmem((2 * N, 8, 256), jnp.int32),
            vmem((2 * N, micro, toks, wg // N), BF16),
            vmem((2 * N, micro, toks, wa // N), BF16),
            vmem((N, N, pgc, kg), BF16),
            vmem((N, N, pa, ka), BF16),
            vmem((micro, N, N, PAIR, wg // N), BF16),
            vmem((micro, N, N, PAIR, wa // N), BF16),
            vmem((micro, N, N, PAIR, kg), BF16),
            vmem((micro, N, N, PAIR, ka), BF16),
            vmem((micro, N, N, PAIR, kg), BF16),
            vmem((micro, N, N, PAIR, ka), BF16),
            vmem((micro, N, PAIR, ka), BF16),
            vmem((micro, N, PAIR, ka), BF16),
            vmem((N * N, rows, kg), F32),
            vmem((N * N, rows, kg), F32),
            dma((32,)),
            dma((2 * N,)),
            dma((2 * N,)),
            dma((micro, 2 * N)),
            dma((micro, 2 * N)),
            dma((6,)),
            dma((3, N)),
            dma((3, 2)),
            dma((3, N, 4)),
            dma((micro, N)),
            dma((micro, N)),
            dma((micro, N)),
            dma((N * N,)),
        ],
        compiler_params=pltpu.CompilerParams(
            collective_id=0, has_side_effects=True, vmem_limit_bytes=63 << 20
        ),
        name="eigen",
    )(expert_ids[..., 0], sequence_ids, activations, gradients, input_basis, output_basis)[None]


def solution(mesh):
    placed = (
        P(None, ("expert", "panel"), None, None),
        P(None, ("expert", "panel"), None, None),
        P(None, ("expert", "panel"), None, None),
        P(None, ("expert", "panel"), None),
        P("expert", "panel", None),
        P("expert", "panel", None),
    )
    return jax.shard_map(
        per_device,
        mesh=mesh,
        in_specs=placed,
        out_specs=P("expert", "panel", None),
        check_vma=False,
    )
```
